128 devices in a mesh: dp: 8 (over x_lo, y), expert: 16 (over x_hi, z, core).
Axes of the slice: x: 4 (x_hi: 2, x_lo: 2; x = x_hi * 2 + x_lo), y: 4, z: 4, core: 2. Of those that a mesh axis runs over, the one named last changes fastest.
Arguments:
- tokens: bfloat16 [65536, 2048], P(('dp', 'expert')), may hold values from -6 to 6
- probe: bfloat16 [65536, 2048], P(('dp', 'expert')), may hold values from -20 to 20
- domain: int32 [65536], P(('dp', 'expert')), may hold values from 0 to 21
- mix: float32 [22], replicated, may hold values from 0.5 to 2
- router: bfloat16 [2048, 32], replicated, may hold values from -0.125 to 0.125
- picks: int32 [128, 32, 40], P(('dp', 'expert')), may hold values from 0 to 511, as said below
- w_gate: bfloat16 [2048, 32, 768], P(None, 'expert'), may hold values from -0.125 to 0.125
- w_up: bfloat16 [2048, 32, 768], P(None, 'expert'), may hold values from -0.125 to 0.125
- w_down: bfloat16 [2048, 32, 768], P(None, 'expert'), may hold values from -0.21875 to 0.21875
Outputs:
- domain_loss: float32 [22], replicated
- router_grad: float32 [2048, 32], replicated
- grad_gate: bfloat16 [2048, 32, 768], P('dp', 'expert')
- grad_up: bfloat16 [2048, 32, 768], P('dp', 'expert')
- grad_down: bfloat16 [2048, 32, 768], P('dp', 'expert')
The draws below stay inside these ranges and needn't reach their ends.
Inputs may be any that keep to these rules, and one draw needn't show every extreme that they name: The 40 picks of one expert on one device are distinct token positions of that device.
All inputs are finite; a program needn't handle non-finite values.
Results may differ from the reference program's by a relative error of at most 0.018.
Values may be sent and summed in bfloat16 or wider, within the bound.
A program may use at most 192 MiB of HBM per device.

```python
import math
import jax
import jax.numpy as jnp
from jax import lax

D = 2048
FF = 768
DOMAINS = 22
TOK_DEV = 512
EXPERTS = 32
CAP = 40
SHARDS = 128
TOKENS = 65536
N_DP = 8
N_EXPERT = 16


def draw_probe(key, part):
    position = jnp.arange(TOKENS, dtype=jnp.float32)[:, None] / TOKENS
    base = jnp.clip(jax.random.normal(key, (TOKENS, D), jnp.float32), -6.0, 6.0)
    values = base * (1.0 + 2.0 * position)
    return values.astype(jnp.bfloat16)


def draw_picks(key, part):
    subkeys = jax.random.split(key, SHARDS * EXPERTS)

    def shuffled(subkey):
        return jax.random.permutation(subkey, TOK_DEV)
    orders = jax.vmap(shuffled)(subkeys)
    return orders[:, :CAP].reshape(SHARDS, EXPERTS, CAP).astype(jnp.int32)


def set_ends(values, stream_key, least, largest):
    longest = values.shape.index(max(values.shape))
    spots = []
    for shift in (0, 1):
        where = [jax.random.randint(jax.random.fold_in(stream_key, axis), (), 0, length) for axis, length in enumerate(values.shape)]
        where[longest] = (where[longest] + shift) % values.shape[longest]
        spots.append(tuple(where))
    return values.at[spots[0]].set(least).at[spots[1]].set(largest)


def shard_levels(own_key, extent, cuts, smallest, high):
    level, own = 1.0, jax.random.fold_in(own_key, 6)
    for dim, parts in cuts:
        heights = jnp.exp(jax.random.uniform(jax.random.fold_in(own, dim), (parts,), jnp.float32, smallest / len(cuts), high / len(cuts)))
        level = level * jnp.repeat(heights, extent[dim] // parts).reshape([-1 if axis == dim else 1 for axis in range(len(extent))])
    return level


def bell_draw(own_key, extent, spread, reach, pieces=(), kind=jnp.bfloat16):
    values = jax.random.normal(own_key, extent, jnp.float32) * spread
    if len(pieces) > 0:
        values = shard_levels(own_key, extent, pieces, -0.22, 0.18) * values
    return jnp.clip(values, min=-reach, max=reach).astype(kind)


def setup_inputs(seed: int = 0) -> dict:
    seeds = jax.random.split(jax.random.key(seed), 10)
    tokens = bell_draw(seeds[0], (TOKENS, D), 1.0, 6.0, ((0, 128),))
    probe = draw_probe(jax.random.fold_in(seeds[9], 71), 0)
    domain = set_ends(jax.random.randint(seeds[2], (TOKENS,), 0, DOMAINS), jax.random.fold_in(seeds[2], 1), 0, DOMAINS - 1).astype(jnp.int32)
    mix = jnp.clip(jnp.exp(jax.random.uniform(seeds[3], (DOMAINS,), jnp.float32, math.log(0.5), math.log(2.0))), 0.5, 2.0)
    router = bell_draw(seeds[4], (D, EXPERTS), D ** -0.5, 0.125)
    picks = draw_picks(jax.random.fold_in(seeds[9], 71), 0)
    w_gate = bell_draw(seeds[6], (D, EXPERTS, FF), D ** -0.5, 0.125, ((1, 16),))
    w_up = bell_draw(seeds[7], (D, EXPERTS, FF), D ** -0.5, 0.125, ((1, 16),))
    w_down = bell_draw(seeds[8], (D, EXPERTS, FF), FF ** -0.5, 0.21875, ((1, 16),))
    return {"tokens": tokens, "probe": probe, "domain": domain, "mix": mix, "router": router, "picks": picks, "w_gate": w_gate, "w_up": w_up, "w_down": w_down}


def rounded(value):
    return lax.optimization_barrier(value.astype(jnp.bfloat16)).astype(jnp.float32)

def expert_pass(tokens_grid, picks, w_gate, w_up, w_down, expert_index):
    shard_ids = jnp.arange(SHARDS, dtype=jnp.int32)[:, None]
    chosen = lax.dynamic_index_in_dim(picks, expert_index, 1, keepdims=False)
    gathered = tokens_grid[shard_ids, chosen]
    grouped = gathered.reshape(N_DP, N_EXPERT * CAP, D).astype(jnp.float32)
    gate_mat = lax.dynamic_index_in_dim(w_gate, expert_index, 1, keepdims=False).astype(jnp.float32)
    up_mat = lax.dynamic_index_in_dim(w_up, expert_index, 1, keepdims=False).astype(jnp.float32)
    down_mat = lax.dynamic_index_in_dim(w_down, expert_index, 1, keepdims=False).astype(jnp.float32)
    pre_gate = jnp.einsum('grd,df->grf', grouped, gate_mat)
    pre_up = jnp.einsum('grd,df->grf', grouped, up_mat)
    hidden = rounded(jax.nn.silu(pre_gate) * pre_up)
    result = rounded(jnp.einsum('grf,df->grd', hidden, down_mat))
    return (chosen, grouped, pre_gate, pre_up, hidden, result, down_mat)

def group_sum(left, right):
    partial_sums = rounded(jnp.einsum('grd,grf->gdf', left, right))
    return lax.optimization_barrier(jnp.sum(partial_sums, axis=0)).astype(jnp.bfloat16)

def reference(tokens, probe, domain, mix, router, picks, w_gate, w_up, w_down):
    tokens_grid = tokens.reshape(SHARDS, TOK_DEV, D)
    shard_ids = jnp.arange(SHARDS, dtype=jnp.int32)[:, None]
    logits = jnp.dot(tokens, router, preferred_element_type=jnp.float32).reshape(SHARDS, TOK_DEV, EXPERTS)
    gate_vals = jax.nn.sigmoid(jnp.take_along_axis(jnp.transpose(logits, (0, 2, 1)), picks, axis=2))
    expert_list = jnp.arange(EXPERTS, dtype=jnp.int32)

    def forward_step(total, expert_index):
        chosen, _, _, _, _, result, _ = expert_pass(tokens_grid, picks, w_gate, w_up, w_down, expert_index)
        gate_one = lax.dynamic_index_in_dim(gate_vals, expert_index, 1, keepdims=False)
        adding = gate_one[:, :, None] * result.reshape(SHARDS, CAP, D)
        return (total.at[shard_ids, chosen].add(adding), None)
    added, _ = lax.scan(forward_step, jnp.zeros((SHARDS, TOK_DEV, D), jnp.float32), expert_list)
    layer_out = tokens_grid.astype(jnp.float32) + added
    difference = layer_out - probe.reshape(SHARDS, TOK_DEV, D).astype(jnp.float32)
    per_token = lax.optimization_barrier(jnp.sum(difference * difference, axis=2))
    member = (domain.reshape(SHARDS, TOK_DEV)[:, :, None] == jnp.arange(DOMAINS, dtype=jnp.int32)[None, None, :]).astype(jnp.float32)
    domain_loss = lax.optimization_barrier(jnp.sum(per_token[:, :, None] * member, axis=(0, 1))) * (DOMAINS / (TOKENS * D))
    loss_scale = 1.0 / math.sqrt(SHARDS * CAP)
    weight_tok = lax.optimization_barrier(jnp.sum(member * mix[None, None, :], axis=2))
    upstream = (loss_scale * weight_tok)[:, :, None] * difference

    def backward_step(expert_index):
        chosen, grouped, pre_gate, pre_up, hidden, result, down_mat = expert_pass(tokens_grid, picks, w_gate, w_up, w_down, expert_index)
        gate_one = lax.dynamic_index_in_dim(gate_vals, expert_index, 1, keepdims=False)
        picked_up = upstream[shard_ids, chosen]
        gate_slope = lax.optimization_barrier(jnp.sum(picked_up * result.reshape(SHARDS, CAP, D), axis=2))
        logit_grad = gate_slope * gate_one * (1.0 - gate_one)
        sending = rounded(gate_one[:, :, None] * picked_up).reshape(N_DP, N_EXPERT * CAP, D)
        hidden_grad = jnp.einsum('grd,df->grf', sending, down_mat)
        sigmoid_gate = jax.nn.sigmoid(pre_gate)
        gate_in = rounded(hidden_grad * pre_up * sigmoid_gate * (1.0 + pre_gate * (1.0 - sigmoid_gate)))
        up_in = rounded(hidden_grad * jax.nn.silu(pre_gate))
        return (group_sum(grouped, gate_in), group_sum(grouped, up_in), group_sum(sending, hidden), logit_grad)
    grad_gate, grad_up, grad_down, logit_grads = lax.map(backward_step, expert_list)
    logit_all = jnp.transpose(logit_grads, (1, 0, 2))
    shard_index = jnp.arange(SHARDS, dtype=jnp.int32)[:, None, None]
    expert_index = jnp.arange(EXPERTS, dtype=jnp.int32)[None, :, None]
    placed = jnp.zeros((SHARDS, TOK_DEV, EXPERTS), jnp.float32).at[shard_index, picks, expert_index].set(logit_all)
    router_grad = jnp.dot(tokens.astype(jnp.float32).T, placed.reshape(TOKENS, EXPERTS), precision=lax.Precision.HIGHEST)
    return (domain_loss, router_grad, jnp.transpose(grad_gate, (1, 0, 2)), jnp.transpose(grad_up, (1, 0, 2)), jnp.transpose(grad_down, (1, 0, 2)))
```

```python
import math

import jax
import jax.numpy as jnp
from jax import lax
from jax.sharding import PartitionSpec as P

BF = jnp.bfloat16
F32 = jnp.float32


def body(tokens, probe, domain, mix, router, picks, w_gate, w_up, w_down):
    token_count, model_width = tokens.shape
    expert_count = router.shape[1]
    slot_count = picks.shape[2]
    pick_count = expert_count * slot_count
    domain_count = mix.shape[0]
    device_count = lax.axis_size("dp") * lax.axis_size("expert")
    flat = picks[0].reshape(pick_count)
    token_ids = jnp.arange(token_count, dtype=jnp.int32)
    select = (flat[:, None] == token_ids[None, :]).astype(BF)
    expert_of = jnp.repeat(jnp.arange(expert_count, dtype=jnp.int32), slot_count)
    own_expert = expert_of[:, None] == jnp.arange(expert_count, dtype=jnp.int32)[None, :]
    outgoing = jnp.dot(select, tokens, preferred_element_type=F32).astype(BF)
    received = lax.all_to_all(
        outgoing.reshape(expert_count, 1, slot_count, model_width),
        "expert", split_axis=0, concat_axis=1, tiled=True,
    )
    logits = jnp.dot(outgoing, router, preferred_element_type=F32)
    gate = jax.nn.sigmoid(jnp.sum(jnp.where(own_expert, logits, 0.0), axis=1))
    pre_gate = jnp.einsum("jsrd,djf->jsrf", received, w_gate, preferred_element_type=F32)
    pre_up = jnp.einsum("jsrd,djf->jsrf", received, w_up, preferred_element_type=F32)
    hidden = (jax.nn.silu(pre_gate) * pre_up).astype(BF)
    result = jnp.einsum("jsrf,djf->jsrd", hidden, w_down, preferred_element_type=F32).astype(BF)
    returned = lax.all_to_all(result, "expert", split_axis=1, concat_axis=0, tiled=True)
    returned = returned.reshape(pick_count, model_width)
    weighted = jnp.where(
        flat[None, :] == token_ids[:, None], gate.astype(BF)[None, :], jnp.zeros((), BF)
    )
    added = jnp.dot(weighted, returned, preferred_element_type=F32)
    difference = tokens.astype(F32) + added - probe.astype(F32)
    per_token = jnp.sum(difference * difference, axis=1)
    member = (domain[:, None] == jnp.arange(domain_count, dtype=jnp.int32)[None, :]).astype(F32)
    local_loss = jnp.sum(per_token[:, None] * member, axis=0)
    loss_scale = 1.0 / math.sqrt(device_count * slot_count)
    weight_tok = jnp.sum(member * mix[None, :], axis=1)
    upstream = ((loss_scale * weight_tok)[:, None] * difference).astype(BF)
    picked_up = jnp.dot(select, upstream, preferred_element_type=F32)
    sending = (gate[:, None] * picked_up).astype(BF)
    gate_slope = jnp.sum(picked_up * returned.astype(F32), axis=1)
    logit_grad = gate_slope * gate * (1.0 - gate)
    placing = jnp.where(own_expert, logit_grad[:, None], 0.0)
    high = placing.astype(BF)
    low = (placing - high.astype(F32)).astype(BF)
    placed = lax.dot_general(
        select, jnp.concatenate([high, low], axis=1), (((0,), (0,)), ((), ())),
        preferred_element_type=F32,
    ).astype(BF)
    router_part = lax.dot_general(
        tokens, placed, (((0,), (0,)), ((), ())), preferred_element_type=F32
    )
    router_part = router_part[:, :expert_count] + router_part[:, expert_count:]
    loss_rows = jnp.zeros((8, expert_count), F32).at[0, :domain_count].set(local_loss)
    summed = lax.psum(jnp.concatenate([router_part, loss_rows], axis=0), ("dp", "expert"))
    back_grad = lax.all_to_all(
        sending.reshape(expert_count, 1, slot_count, model_width),
        "expert", split_axis=0, concat_axis=1, tiled=True,
    )

    def reduced(left, right):
        part = jnp.einsum("jsrd,jsrf->djf", left, right, preferred_element_type=F32)
        return lax.psum_scatter(part.astype(BF), "dp", scatter_dimension=0, tiled=True)

    grad_down = reduced(back_grad, hidden)
    hidden_grad = jnp.einsum("jsrd,djf->jsrf", back_grad, w_down, preferred_element_type=F32)
    sigmoid_gate = jax.nn.sigmoid(pre_gate)
    gate_in = (
        hidden_grad * pre_up * sigmoid_gate * (1.0 + pre_gate * (1.0 - sigmoid_gate))
    ).astype(BF)
    up_in = (hidden_grad * (pre_gate * sigmoid_gate)).astype(BF)
    grad_gate = reduced(received, gate_in)
    grad_up = reduced(received, up_in)
    domain_loss = summed[model_width, :domain_count] * (
        domain_count / (token_count * device_count * model_width)
    )
    return (domain_loss, summed[:model_width], grad_gate, grad_up, grad_down)


def solution(mesh):
    placed = (
        P(("dp", "expert"), None),
        P(("dp", "expert"), None),
        P(("dp", "expert")),
        P(),
        P(),
        P(("dp", "expert"), None, None),
        P(None, "expert", None),
        P(None, "expert", None),
        P(None, "expert", None),
    )
    return jax.shard_map(
        body,
        mesh=mesh,
        in_specs=placed,
        out_specs=(
            P(),
            P(),
            P("dp", "expert", None),
            P("dp", "expert", None),
            P("dp", "expert", None),
        ),
        check_vma=False,
    )
```
